32 devices in a mesh: shard: 4 (over z), tensor: 4 (over x, core), dp: 2 (over y).
Axes of the slice: x: 2, y: 2, z: 4, core: 2. Of those that a mesh axis runs over, the one named last changes fastest.
Arguments:
- gradient: bfloat16 [1, 8192, 8192], P(None, 'shard', ('tensor', 'dp')), may hold values from -16 to 16
- momentum: float32 [1, 8192, 8192], P(None, 'shard', ('tensor', 'dp')), may hold values from -16 to 16
- prior_right_factor: float32 [1, 8192, 128], P(None, ('tensor', 'dp')), may hold values from -8 to 8
Outputs:
- momentum_next: float32 [1, 8192, 8192], P(None, 'shard', ('tensor', 'dp'))
- following_right_factor: float32 [1, 8192, 128], P(None, ('tensor', 'dp'))
- direction: bfloat16 [1, 8192, 8192], P(None, 'shard', ('tensor', 'dp'))
The draws below stay inside these ranges and needn't reach their ends.
All inputs are finite; a program needn't handle non-finite values.
Results may differ from the reference program's by a relative error of at most 0.0029.
Values sent between devices are 32-bit elements; how exact they have to be, the bound alone decides.
A program may use at most 64 MiB of HBM per device.

```python
import math
import jax
import jax.numpy as jnp
from jax import lax

M = 8192
N = 8192
R = 128
LAYERS = 1


def orthonormal_columns(seed_key, row_count, col_count):
    gaussian = jax.random.normal(seed_key, (LAYERS, row_count, col_count), jnp.float32)

    def orthonormalize(matrix):
        q_matrix, r_matrix = jnp.linalg.qr(matrix)
        return q_matrix
    return jax.vmap(orthonormalize)(gaussian)


def shared_factors(key):
    left_vectors = jax.random.normal(jax.random.fold_in(key, 11), (LAYERS, M, R), jnp.float32) / math.sqrt(M)
    joint_columns = orthonormal_columns(jax.random.fold_in(key, 12), N, 2 * R)
    mixing = orthonormal_columns(jax.random.fold_in(key, 13), R, R)
    positions = jnp.arange(R, dtype=jnp.float32) / max(R - 1, 1)
    jitter = jax.random.uniform(jax.random.fold_in(key, 14), (LAYERS, R), jnp.float32, 0.9, 1.1)
    strengths = jnp.power(2000.0, -positions)[None, :] * jitter
    strengths = strengths * (0.95 * math.sqrt(M * N) / jnp.sqrt(jnp.sum(strengths * strengths, axis=1, keepdims=True)))
    momentum_share = jax.random.uniform(jax.random.fold_in(key, 15), (LAYERS, R), jnp.float32, 0.55, 0.9)
    row_scales = jnp.ones((LAYERS, M), jnp.float32)
    return (left_vectors, joint_columns, mixing, strengths, momentum_share, row_scales)


def blended_piece(key, stream_tag, use_share, tail_scale):
    left_vectors, joint_columns, mixing, strengths, momentum_share, row_scales = shared_factors(key)
    singular_vectors = joint_columns[:, :, :R]
    if use_share:
        weights = momentum_share
    else:
        weights = 1.0 - momentum_share
    rescaled_update = left_vectors * (strengths * weights)[:, None, :]
    rank_limited = jnp.einsum('fwd,fad->fwa', rescaled_update, singular_vectors, precision=lax.Precision.HIGHEST)
    noise_key = jax.random.fold_in(key, stream_tag)
    random_perturbation = jax.random.normal(noise_key, (LAYERS, M, N), jnp.float32)
    basis_component = jnp.einsum('aph,aht->apt', random_perturbation, joint_columns, precision=lax.Precision.HIGHEST)
    residual_portion = random_perturbation - jnp.einsum('fwd,fad->fwa', basis_component, joint_columns, precision=lax.Precision.HIGHEST)
    return row_scales[:, :, None] * (rank_limited + tail_scale * residual_portion)


def draw_momentum(key, part):
    return jnp.clip(blended_piece(key, 21, True, 0.08), -16.0, 16.0)


def draw_gradient(key, part):
    return jnp.clip(blended_piece(key, 22, False, 0.06), -16.0, 16.0).astype(jnp.bfloat16)


def draw_prior_right_factor(key, part):
    left_vectors, joint_columns, mixing, strengths, momentum_share, row_scales = shared_factors(key)
    singular_vectors = joint_columns[:, :, :R]
    other_vectors = joint_columns[:, :, R:]
    aligned = jnp.einsum('lnr,lrs->lns', singular_vectors, mixing, precision=lax.Precision.HIGHEST)
    tilt = math.sqrt(0.5)
    factor = math.sqrt(N) * (tilt * aligned + tilt * other_vectors)
    return jnp.clip(factor, -8.0, 8.0)


def setup_inputs(seed: int = 0) -> dict:
    keys = jax.random.split(jax.random.key(seed), 4)
    return {
        "gradient": draw_gradient(jax.random.fold_in(keys[3], 71), 0),
        "momentum": draw_momentum(jax.random.fold_in(keys[3], 71), 0),
        "prior_right_factor": draw_prior_right_factor(jax.random.fold_in(keys[3], 71), 0),
    }


decay_rate = 0.95
epsilon = 1e-06

def one_layer(operands):
    gradient, momentum, prior_right_factor = operands
    mixed_update = momentum + gradient.astype(jnp.float32)
    left = jnp.dot(mixed_update, prior_right_factor, precision=lax.Precision.HIGHEST)
    q_matrix, r_matrix = jnp.linalg.qr(left)
    column_basis = q_matrix * jnp.sign(jnp.diagonal(r_matrix))[None, :]
    fresh_right_factor = jnp.dot(mixed_update.T, column_basis, precision=lax.Precision.HIGHEST)
    momentum_next = mixed_update - (1.0 - decay_rate) * jnp.dot(column_basis, fresh_right_factor.T, precision=lax.Precision.HIGHEST)
    scales = jnp.sqrt(lax.optimization_barrier(jnp.mean(fresh_right_factor * fresh_right_factor, axis=0)) + epsilon)
    following_right_factor = fresh_right_factor / scales[None, :]
    direction = (jnp.sqrt(M / R) * jnp.dot(column_basis, following_right_factor.T, precision=lax.Precision.HIGHEST)).astype(jnp.bfloat16)
    return (momentum_next, following_right_factor, direction)

def reference(gradient, momentum, prior_right_factor):
    momentum_next, following_right_factor, direction = lax.map(one_layer, (gradient, momentum, prior_right_factor))
    return (momentum_next, following_right_factor, direction)
```

```python
import functools

import jax
import jax.numpy as jnp
from jax import lax
from jax.experimental import pallas as pl
from jax.experimental.pallas import tpu as pltpu
from jax.sharding import PartitionSpec as P

MESH = pl.DeviceIdType.MESH
HIGHEST = lax.Precision.HIGHEST
decay_rate = 0.95
epsilon = 1e-06
CHUNKS = 8


def dot(a, b, dims, precision=HIGHEST):
    return lax.dot_general(
        a, b, (dims, ((), ())), precision=precision, preferred_element_type=jnp.float32
    )


def split(value):
    high = value.astype(jnp.bfloat16)
    low = (value - high.astype(jnp.float32)).astype(jnp.bfloat16)
    return high, low


def inverse_factor(gram):
    size = gram.shape[0]
    sub = lax.broadcasted_iota(jnp.int32, (8, size), 0)
    lane = lax.broadcasted_iota(jnp.int32, (8, size), 1)
    rows = lax.broadcasted_iota(jnp.int32, (size, size), 0)
    lanes = lax.broadcasted_iota(jnp.int32, (size, size), 1)

    def row(value, index):
        return jnp.broadcast_to(value[index : index + 1], value.shape)

    def block(step, a):
        top = a[:8]
        columns = [jnp.broadcast_to(top[:, c : c + 1], (8, size)) for c in range(8)]
        panel = jnp.where(lane < 8, jnp.where(lane == sub, 1.0, 0.0), top)
        scale = jnp.zeros((8, size), jnp.float32)
        for c in range(8):
            inverse_root = lax.rsqrt(row(columns[c], c))
            scale = jnp.where(sub == c, inverse_root, scale)
            factor = jnp.where(sub > c, columns[c] * (inverse_root * inverse_root), 0.0)
            panel = panel - factor * row(panel, c)
            for j in range(c + 1, 8):
                columns[j] = columns[j] - factor * row(columns[j], c)
        square = scale * scale
        solved = panel * square
        for c in range(7, 0, -1):
            solved = solved - jnp.where(sub < c, columns[c] * square, 0.0) * row(solved, c)
        active = rows < size - 8 * step
        source = jnp.where(active, a, 0.0)[8:]
        rest = jnp.where(active & (lanes < 8), 0.0, a)[8:]
        for c in range(8):
            rest = rest - jnp.broadcast_to(source[:, c : c + 1], rest.shape) * jnp.broadcast_to(
                solved[c : c + 1], rest.shape
            )
        return pltpu.roll(jnp.concatenate([rest, panel * scale], axis=0), size - 8, 1)

    return jnp.where(rows >= lanes, lax.fori_loop(0, size // 8, block, gram), 0.0)


class Group:
    def __init__(self, count, me, where):
        self.count, self.me, self.where = count, me, where

    def peer(self, k):
        other = lax.rem(self.me + k, self.count)
        return other, self.where(other)


def groups(shape):
    s, t, d = lax.axis_index("shard"), lax.axis_index("tensor"), lax.axis_index("dp")
    tensor, dp = shape["tensor"], shape["dp"]
    cores = 2 if tensor % 2 == 0 else 1
    core, x = lax.rem(t, cores), lax.div(t, cores)
    return {
        "core": Group(cores, core, lambda j: {"tensor": x * cores + j}),
        "x": Group(tensor // cores, x, lambda j: {"tensor": j * cores + core}),
        "y": Group(dp, d, lambda j: {"dp": j}),
        "z": Group(shape["shard"], s, lambda j: {"shard": j}),
        "plane": Group(
            tensor * dp, t * dp + d, lambda j: {"tensor": lax.div(j, dp), "dp": lax.rem(j, dp)}
        ),
    }


def stage_plan(shape, rows):
    cores = 2 if shape["tensor"] % 2 == 0 else 1
    sizes = {"core": cores, "x": shape["tensor"] // cores, "y": shape["dp"]}
    members = shape["tensor"] * shape["dp"]
    halves = 2 if rows % (16 * members) == 0 else 1
    orders = (("core", "x", "y"), ("core", "y", "x"))[:halves]
    return sizes, halves, orders


def factors(shape, momentum_ref, gradient_ref, prior_ref, basis_ref, right_ref, following_ref, *scratch):
    (mixed, raw, left, whole, local, grams, shares, share_in, squares, load_sem, gram_send, gram_recv, share_send,
     share_recv, full_send, full_recv, square_send, square_recv, *stages) = scratch
    rows, cols = mixed.shape
    rank = prior_ref.shape[1]
    where = groups(shape)
    sizes, halves, orders = stage_plan(shape, rows)
    part = rows // CHUNKS

    def load(i):
        at = pl.ds(pl.multiple_of(i * part, 8), part)
        return (
            pltpu.make_async_copy(momentum_ref.at[at], mixed.at[at], load_sem.at[0, i]),
            pltpu.make_async_copy(gradient_ref.at[at], raw.at[at], load_sem.at[1, i]),
        )

    for i in range(CHUNKS):
        for copy in load(i):
            copy.start()

    barrier = pltpu.get_barrier_semaphore()
    peers = 0
    for name in ("plane", "z"):
        for k in range(1, where[name].count):
            pl.semaphore_signal(barrier, inc=1, device_id=where[name].peer(k)[1], device_id_type=MESH)
            peers += 1
    pl.semaphore_wait(barrier, peers)

    prior = prior_ref[...]

    def first(i, carry):
        for copy in load(i):
            copy.wait()
        at = pl.ds(pl.multiple_of(i * part, 8), part)
        value = mixed[at, :] + raw[at, :].astype(jnp.float32)
        mixed[at, :] = value
        left[at, :] = dot(value, prior, ((1,), (0,)))
        return carry

    lax.fori_loop(0, CHUNKS, first, 0)

    starts = [h * (rows // halves) for h in range(halves)]
    sizes_now = [rows // halves] * halves
    trail = []
    for level in range(3):
        pending = []
        for h in range(halves):
            name = orders[h][level]
            group = where[name]
            buffer, send_sem, recv_sem = stages[level * 6 + h * 3 : level * 6 + h * 3 + 3] if halves == 2 else stages[level * 3 : level * 3 + 3]
            if group.count == 1:
                continue
            size = sizes_now[h] // group.count
            copies = []
            for k in range(1, group.count):
                other, device = group.peer(k)
                copy = pltpu.make_async_remote_copy(
                    src_ref=left.at[pl.ds(pl.multiple_of(starts[h] + other * size, 8), size)],
                    dst_ref=buffer.at[k - 1],
                    send_sem=send_sem.at[k - 1],
                    recv_sem=recv_sem.at[k - 1],
                    device_id=device,
                    device_id_type=MESH,
                )
                copy.start()
                copies.append(copy)
            pending.append((h, group, size, copies, buffer))
        for h, group, size, copies, buffer in pending:
            for copy in copies:
                copy.wait()
            own = pl.multiple_of(starts[h] + group.me * size, 8)
            total = left[pl.ds(own, size), :]
            for k in range(group.count - 1):
                total = total + buffer[k]
            left[pl.ds(own, size), :] = total
            starts[h], sizes_now[h] = own, size
            trail.append((level, h, group, own, size))
    for h in range(halves):
        own = pl.ds(starts[h], sizes_now[h])
        whole[own, :] = left[own, :]
    for level in (2, 1, 0):
        copies = []
        for stage, h, group, own, size in trail:
            if stage != level:
                continue
            index = (level * 2 + h) if halves == 2 else level
            for k in range(1, group.count):
                other, device = group.peer(k)
                at = pl.ds(own, size)
                copy = pltpu.make_async_remote_copy(
                    src_ref=whole.at[at],
                    dst_ref=whole.at[at],
                    send_sem=full_send.at[index, k - 1],
                    recv_sem=full_recv.at[index, k - 1],
                    device_id=device,
                    device_id_type=MESH,
                )
                copy.start()
                copies.append(copy)
        for copy in copies:
            copy.wait()

    def exchange(slots, group, send_sem, recv_sem):
        copies = []
        for k in range(1, group.count):
            copy = pltpu.make_async_remote_copy(
                src_ref=slots.at[group.me],
                dst_ref=slots.at[group.me],
                send_sem=send_sem.at[k - 1],
                recv_sem=recv_sem.at[k - 1],
                device_id=group.peer(k)[1],
                device_id_type=MESH,
            )
            copy.start()
            copies.append(copy)
        return copies

    def summed(slots, count):
        total = slots[0]
        for i in range(1, count):
            total = total + slots[i]
        return total

    z = where["z"]
    value = whole[...]
    grams[0, z.me] = dot(value, value, ((0,), (0,)))
    for copy in exchange(grams.at[0], z, gram_send.at[0], gram_recv.at[0]):
        copy.wait()
    inverse = inverse_factor(summed(grams.at[0], z.count))
    value = dot(whole[...], inverse, ((1,), (1,)))
    basis_ref[...] = value
    grams[1, z.me] = dot(value, value, ((0,), (0,)))
    gram_copies = exchange(grams.at[1], z, gram_send.at[1], gram_recv.at[1])

    local[...] = dot(value, mixed[...], ((0,), (0,)))
    share = rank // z.count
    share_copies = []
    for k in range(1, z.count):
        other, device = z.peer(k)
        copy = pltpu.make_async_remote_copy(
            src_ref=local.at[pl.ds(pl.multiple_of(other * share, 8), share)],
            dst_ref=share_in.at[k - 1],
            send_sem=share_send.at[k - 1],
            recv_sem=share_recv.at[k - 1],
            device_id=device,
            device_id_type=MESH,
        )
        copy.start()
        share_copies.append(copy)
    for copy in gram_copies:
        copy.wait()
    inverse = inverse_factor(summed(grams.at[1], z.count))
    for copy in share_copies:
        copy.wait()
    total = local[pl.ds(pl.multiple_of(z.me * share, 8), share), :]
    for k in range(z.count - 1):
        total = total + share_in[k]
    shares[z.me] = total
    full = exchange(shares, z, full_send.at[full_send.shape[0] - 1], full_recv.at[full_recv.shape[0] - 1])
    basis_ref[...] = dot(basis_ref[...], inverse, ((1,), (1,)))
    for copy in full:
        copy.wait()
    stacked = jnp.concatenate([shares[i] for i in range(z.count)], axis=0)
    right = dot(stacked, inverse, ((0,), (1,)))
    right_ref[...] = right
    plane = where["plane"]
    squares[plane.me] = jnp.broadcast_to(jnp.sum(right * right, axis=0, keepdims=True), (8, rank))
    for copy in exchange(squares, plane, square_send, square_recv):
        copy.wait()
    mean = summed(squares, plane.count)[:1] / (cols * plane.count)
    following_ref[...] = right / jnp.sqrt(mean + epsilon)


def finish(scale, momentum_ref, gradient_ref, basis_ref, right_ref, following_ref, next_ref, direction_ref):
    high, low = split(basis_ref[...])
    right = right_ref[...].astype(jnp.bfloat16)
    follow_high, follow_low = split(following_ref[...])
    dims = ((1,), (1,))
    next_ref[...] = (
        momentum_ref[...]
        + gradient_ref[...].astype(jnp.float32)
        - (1.0 - decay_rate) * dot(high, right, dims, None)
    )
    product = dot(high, follow_high, dims, None) + (
        dot(high, follow_low, dims, None) + dot(low, follow_high, dims, None)
    )
    direction_ref[...] = (scale * product).astype(jnp.bfloat16)


def shards(shape, gradient, momentum, prior_right_factor):
    gradient, momentum, prior = gradient[0], momentum[0], prior_right_factor[0]
    rows, cols = momentum.shape
    rank = prior.shape[1]
    sizes, halves, orders = stage_plan(shape, rows)
    stages = []
    now = [rows // halves] * halves
    widest = max(max(sizes.values()), shape["shard"], 2) - 1
    for level in range(3):
        for h in range(halves):
            count = sizes[orders[h][level]]
            now[h] //= count
            stages += [
                pltpu.VMEM((max(count - 1, 1), now[h], rank), jnp.float32),
                pltpu.SemaphoreType.DMA((max(count - 1, 1),)),
                pltpu.SemaphoreType.DMA((max(count - 1, 1),)),
            ]
    z = shape["shard"]
    plane = shape["tensor"] * shape["dp"]
    dma = pltpu.SemaphoreType.DMA
    vmem = pl.BlockSpec(memory_space=pltpu.VMEM)
    anywhere = pl.BlockSpec(memory_space=pl.ANY)
    f32 = jnp.float32
    basis, right, following = pl.pallas_call(
        functools.partial(factors, shape),
        out_shape=[
            jax.ShapeDtypeStruct((rows, rank), f32),
            jax.ShapeDtypeStruct((cols, rank), f32),
            jax.ShapeDtypeStruct((cols, rank), f32),
        ],
        in_specs=[anywhere, anywhere, vmem],
        out_specs=[vmem, vmem, vmem],
        scratch_shapes=[
            pltpu.VMEM((rows, cols), f32),
            pltpu.VMEM((rows, cols), jnp.bfloat16),
            pltpu.VMEM((rows, rank), f32),
            pltpu.VMEM((rows, rank), f32),
            pltpu.VMEM((rank, cols), f32),
            pltpu.VMEM((2, z, rank, rank), f32),
            pltpu.VMEM((z, rank // z, cols), f32),
            pltpu.VMEM((max(z - 1, 1), rank // z, cols), f32),
            pltpu.VMEM((plane, 8, rank), f32),
            dma((2, CHUNKS)),
            dma((2, max(z - 1, 1))),
            dma((2, max(z - 1, 1))),
            dma((max(z - 1, 1),)),
            dma((max(z - 1, 1),)),
            dma((3 * halves + 1, widest)),
            dma((3 * halves + 1, widest)),
            dma((max(plane - 1, 1),)),
            dma((max(plane - 1, 1),)),
            *stages,
        ],
        compiler_params=pltpu.CompilerParams(
            collective_id=0, has_side_effects=True, vmem_limit_bytes=48 * 1024 * 1024
        ),
        name="factors",
    )(momentum, gradient, prior)

    block = rows // CHUNKS
    wide = pl.BlockSpec((block, cols), lambda i: (i, 0))
    whole = pl.BlockSpec((cols, rank), lambda i: (0, 0))
    scale = float((rows * z / rank) ** 0.5)
    momentum_next, direction = pl.pallas_call(
        functools.partial(finish, scale),
        grid=(CHUNKS,),
        out_shape=[
            jax.ShapeDtypeStruct((rows, cols), f32),
            jax.ShapeDtypeStruct((rows, cols), jnp.bfloat16),
        ],
        in_specs=[wide, wide, pl.BlockSpec((block, rank), lambda i: (i, 0)), whole, whole],
        out_specs=[wide, wide],
        name="finish",
    )(momentum, gradient, basis, right, following)
    return momentum_next[None], following[None], direction[None]


def solution(mesh):
    return jax.shard_map(
        functools.partial(shards, dict(mesh.shape)),
        mesh=mesh,
        in_specs=(
            P(None, "shard", ("tensor", "dp")),
            P(None, "shard", ("tensor", "dp")),
            P(None, ("tensor", "dp"), None),
        ),
        out_specs=(
            P(None, "shard", ("tensor", "dp")),
            P(None, ("tensor", "dp"), None),
            P(None, "shard", ("tensor", "dp")),
        ),
        check_vma=False,
    )
```

```python
import functools

import jax
import jax.numpy as jnp
from jax import lax
from jax.experimental import pallas as pl
from jax.experimental.pallas import tpu as pltpu
from jax.sharding import PartitionSpec as P

MESH = pl.DeviceIdType.MESH
HIGHEST = lax.Precision.HIGHEST
decay_rate = 0.95
epsilon = 1e-06
CHUNKS = 8


def dot(a, b, dims, precision=HIGHEST):
    return lax.dot_general(
        a, b, (dims, ((), ())), precision=precision, preferred_element_type=jnp.float32
    )


def split(value):
    high = value.astype(jnp.bfloat16)
    low = (value - high.astype(jnp.float32)).astype(jnp.bfloat16)
    return high, low


def product(lhs, rhs):
    high, low = split(lhs)
    pair = jnp.concatenate(split(rhs), axis=1)
    both = dot(high, pair, ((1,), (0,)), None) + dot(low, pair, ((1,), (0,)), None)
    width = rhs.shape[1]
    return both[:, :width] + both[:, width:]


def inverse_factor(gram):
    size = gram.shape[0]
    sub = lax.broadcasted_iota(jnp.int32, (8, size), 0)
    lane = lax.broadcasted_iota(jnp.int32, (8, size), 1)
    rows = lax.broadcasted_iota(jnp.int32, (size, size), 0)
    lanes = lax.broadcasted_iota(jnp.int32, (size, size), 1)

    def row(value, index):
        return jnp.broadcast_to(value[index : index + 1], value.shape)

    def block(step, a):
        top = a[:8]
        columns = [jnp.broadcast_to(top[:, c : c + 1], (8, size)) for c in range(8)]
        panel = jnp.where(lane < 8, jnp.where(lane == sub, 1.0, 0.0), top)
        scale = jnp.zeros((8, size), jnp.float32)
        for c in range(8):
            inverse_root = lax.rsqrt(row(columns[c], c))
            scale = jnp.where(sub == c, inverse_root, scale)
            factor = jnp.where(sub > c, columns[c] * (inverse_root * inverse_root), 0.0)
            panel = panel - factor * row(panel, c)
            for j in range(c + 1, 8):
                columns[j] = columns[j] - factor * row(columns[j], c)
        square = scale * scale
        solved = panel * square
        for c in range(7, 0, -1):
            solved = solved - jnp.where(sub < c, columns[c] * square, 0.0) * row(solved, c)
        active = rows < size - 8 * step
        source = jnp.where(active, a, 0.0)[8:]
        rest = jnp.where(active & (lanes < 8), 0.0, a)[8:]
        for c in range(8):
            rest = rest - jnp.broadcast_to(source[:, c : c + 1], rest.shape) * jnp.broadcast_to(
                solved[c : c + 1], rest.shape
            )
        return pltpu.roll(jnp.concatenate([rest, panel * scale], axis=0), size - 8, 1)

    return jnp.where(rows >= lanes, lax.fori_loop(0, size // 8, block, gram), 0.0)


class Group:
    def __init__(self, count, me, where):
        self.count, self.me, self.where = count, me, where

    def peer(self, k):
        other = lax.rem(self.me + k, self.count)
        return other, self.where(other)


def groups(shape):
    s, t, d = lax.axis_index("shard"), lax.axis_index("tensor"), lax.axis_index("dp")
    tensor, dp = shape["tensor"], shape["dp"]
    cores = 2 if tensor % 2 == 0 else 1
    core, x = lax.rem(t, cores), lax.div(t, cores)
    return {
        "core": Group(cores, core, lambda j: {"tensor": x * cores + j}),
        "x": Group(tensor // cores, x, lambda j: {"tensor": j * cores + core}),
        "y": Group(dp, d, lambda j: {"dp": j}),
        "z": Group(shape["shard"], s, lambda j: {"shard": j}),
        "plane": Group(
            tensor * dp, t * dp + d, lambda j: {"tensor": lax.div(j, dp), "dp": lax.rem(j, dp)}
        ),
    }


def stage_plan(shape, rows):
    cores = 2 if shape["tensor"] % 2 == 0 else 1
    sizes = {"core": cores, "x": shape["tensor"] // cores, "y": shape["dp"]}
    members = shape["tensor"] * shape["dp"]
    halves = 2 if rows % (16 * members) == 0 else 1
    orders = (("core", "x", "y"), ("core", "y", "x"))[:halves]
    return sizes, halves, orders


def factors(shape, momentum_ref, gradient_ref, prior_ref, basis_ref, right_ref, following_ref, *scratch):
    (mixed, raw, left, whole, local, pieces, piece_in, piece_z, piece_all, shares, share_in, squares, load_sem,
     gram_send, gram_recv, share_send,
     share_recv, full_send, full_recv, square_send, square_recv, *stages) = scratch
    rows, cols = mixed.shape
    rank = prior_ref.shape[1]
    where = groups(shape)
    sizes, halves, orders = stage_plan(shape, rows)
    part = rows // CHUNKS

    def load(i):
        at = pl.ds(pl.multiple_of(i * part, 8), part)
        return (
            pltpu.make_async_copy(momentum_ref.at[at], mixed.at[at], load_sem.at[0, i]),
            pltpu.make_async_copy(gradient_ref.at[at], raw.at[at], load_sem.at[1, i]),
        )

    for i in range(CHUNKS):
        for copy in load(i):
            copy.start()

    barrier = pltpu.get_barrier_semaphore()
    peers = 0
    for name in ("plane", "z"):
        for k in range(1, where[name].count):
            pl.semaphore_signal(barrier, inc=1, device_id=where[name].peer(k)[1], device_id_type=MESH)
            peers += 1
    pl.semaphore_wait(barrier, peers)

    plane, z = where["plane"], where["z"]
    piece = rank // plane.count

    def summed(slots, count):
        total = slots[0]
        for i in range(1, count):
            total = total + slots[i]
        return total

    def sends(group, turn, stage, source, target):
        copies = []
        for k in range(1, group.count):
            other, device = group.peer(k)
            copy = pltpu.make_async_remote_copy(
                src_ref=source(other),
                dst_ref=target,
                send_sem=gram_send.at[turn, stage, k - 1],
                recv_sem=gram_recv.at[turn, stage, k - 1],
                device_id=device,
                device_id_type=MESH,
            )
            copy.start()
            copies.append(copy)
        return copies

    def gram_steps(turn, values):
        gram = sum(dot(value, value, ((0,), (0,))) for value in values)
        for i in range(plane.count):
            pieces[turn, i] = gram[i * piece : (i + 1) * piece]
        piece_in[turn, plane.me] = pieces[turn, plane.me]
        copies = sends(plane, turn, 0, lambda i: pieces.at[turn, i], piece_in.at[turn, plane.me])
        yield
        for copy in copies:
            copy.wait()
        piece_z[turn, z.me] = summed(piece_in.at[turn], plane.count)
        own = piece_z.at[turn, z.me]
        copies = sends(z, turn, 1, lambda i: own, own)
        yield
        for copy in copies:
            copy.wait()
        piece_all[turn, plane.me] = summed(piece_z.at[turn], z.count)
        own = piece_all.at[turn, plane.me]
        copies = sends(plane, turn, 2, lambda i: own, own)
        yield
        for copy in copies:
            copy.wait()
        yield jnp.concatenate([piece_all[turn, i] for i in range(plane.count)], axis=0)

    prior = prior_ref[...]

    def first(i, carry):
        for copy in load(i):
            copy.wait()
        at = pl.ds(pl.multiple_of(i * part, 8), part)
        value = mixed[at, :] + raw[at, :].astype(jnp.float32)
        mixed[at, :] = value
        left[at, :] = product(value, prior)
        return carry

    lax.fori_loop(0, CHUNKS, first, 0)

    starts = [h * (rows // halves) for h in range(halves)]
    sizes_now = [rows // halves] * halves
    trail = []
    for level in range(3):
        pending = []
        for h in range(halves):
            name = orders[h][level]
            group = where[name]
            buffer, send_sem, recv_sem = stages[level * 6 + h * 3 : level * 6 + h * 3 + 3] if halves == 2 else stages[level * 3 : level * 3 + 3]
            if group.count == 1:
                continue
            size = sizes_now[h] // group.count
            copies = []
            for k in range(1, group.count):
                other, device = group.peer(k)
                copy = pltpu.make_async_remote_copy(
                    src_ref=left.at[pl.ds(pl.multiple_of(starts[h] + other * size, 8), size)],
                    dst_ref=buffer.at[k - 1],
                    send_sem=send_sem.at[k - 1],
                    recv_sem=recv_sem.at[k - 1],
                    device_id=device,
                    device_id_type=MESH,
                )
                copy.start()
                copies.append(copy)
            pending.append((h, group, size, copies, buffer))
        for h, group, size, copies, buffer in pending:
            for copy in copies:
                copy.wait()
            own = pl.multiple_of(starts[h] + group.me * size, 8)
            total = left[pl.ds(own, size), :]
            for k in range(group.count - 1):
                total = total + buffer[k]
            left[pl.ds(own, size), :] = total
            starts[h], sizes_now[h] = own, size
            trail.append((level, h, group, own, size))
    for h in range(halves):
        own = pl.ds(starts[h], sizes_now[h])
        whole[own, :] = left[own, :]
    for level in (2, 1, 0):
        copies = []
        for stage, h, group, own, size in trail:
            if stage != level:
                continue
            index = (level * 2 + h) if halves == 2 else level
            for k in range(1, group.count):
                other, device = group.peer(k)
                at = pl.ds(own, size)
                copy = pltpu.make_async_remote_copy(
                    src_ref=whole.at[at],
                    dst_ref=whole.at[at],
                    send_sem=full_send.at[index, k - 1],
                    recv_sem=full_recv.at[index, k - 1],
                    device_id=device,
                    device_id_type=MESH,
                )
                copy.start()
                copies.append(copy)
        if level == 2:
            steps = gram_steps(0, [left[pl.ds(starts[h], sizes_now[h]), :] for h in range(halves)])
            next(steps)
        elif level == 1:
            next(steps)
        else:
            next(steps)
            inverse = inverse_factor(next(steps))
            owned = [
                dot(left[pl.ds(starts[h], sizes_now[h]), :], inverse, ((1,), (1,))) for h in range(halves)
            ]
            steps = gram_steps(1, owned)
            next(steps)
        for copy in copies:
            copy.wait()

    def exchange(slots, group, send_sem, recv_sem):
        copies = []
        for k in range(1, group.count):
            copy = pltpu.make_async_remote_copy(
                src_ref=slots.at[group.me],
                dst_ref=slots.at[group.me],
                send_sem=send_sem.at[k - 1],
                recv_sem=recv_sem.at[k - 1],
                device_id=group.peer(k)[1],
                device_id_type=MESH,
            )
            copy.start()
            copies.append(copy)
        return copies

    value = dot(whole[...], inverse, ((1,), (1,)))
    basis_ref[...] = value
    next(steps)
    high, low = split(value)
    half = cols // 2
    for c in range(2):
        wide_high, wide_low = split(mixed[:, c * half : (c + 1) * half])
        both = dot(jnp.concatenate([high, low], axis=1), wide_high, ((0,), (0,)), None)
        local[:, c * half : (c + 1) * half] = (
            both[:rank] + both[rank:] + dot(high, wide_low, ((0,), (0,)), None)
        )
        if c == 0:
            next(steps)
    share = rank // z.count
    share_copies = []
    for k in range(1, z.count):
        other, device = z.peer(k)
        copy = pltpu.make_async_remote_copy(
            src_ref=local.at[pl.ds(pl.multiple_of(other * share, 8), share)],
            dst_ref=share_in.at[k - 1],
            send_sem=share_send.at[k - 1],
            recv_sem=share_recv.at[k - 1],
            device_id=device,
            device_id_type=MESH,
        )
        copy.start()
        share_copies.append(copy)
    inverse = inverse_factor(next(steps))
    for copy in share_copies:
        copy.wait()
    total = local[pl.ds(pl.multiple_of(z.me * share, 8), share), :]
    for k in range(z.count - 1):
        total = total + share_in[k]
    shares[z.me] = total
    full = exchange(shares, z, full_send.at[full_send.shape[0] - 1], full_recv.at[full_recv.shape[0] - 1])
    basis_ref[...] = dot(basis_ref[...], inverse, ((1,), (1,)))
    for copy in full:
        copy.wait()
    stacked = jnp.concatenate([shares[i] for i in range(z.count)], axis=0)
    right = dot(stacked, inverse, ((0,), (1,)))
    right_ref[...] = right
    squares[plane.me] = jnp.broadcast_to(jnp.sum(right * right, axis=0, keepdims=True), (8, rank))
    for copy in exchange(squares, plane, square_send, square_recv):
        copy.wait()
    mean = summed(squares, plane.count)[:1] / (cols * plane.count)
    following_ref[...] = right / jnp.sqrt(mean + epsilon)


def finish(scale, momentum_ref, gradient_ref, basis_ref, right_ref, following_ref, next_ref, direction_ref):
    high, low = split(basis_ref[...])
    right = right_ref[...].astype(jnp.bfloat16)
    follow_high, follow_low = split(following_ref[...])
    dims = ((1,), (1,))
    next_ref[...] = (
        momentum_ref[...]
        + gradient_ref[...].astype(jnp.float32)
        - (1.0 - decay_rate) * dot(high, right, dims, None)
    )
    product = dot(high, follow_high, dims, None) + (
        dot(high, follow_low, dims, None) + dot(low, follow_high, dims, None)
    )
    direction_ref[...] = (scale * product).astype(jnp.bfloat16)


def shards(shape, gradient, momentum, prior_right_factor):
    gradient, momentum, prior = gradient[0], momentum[0], prior_right_factor[0]
    rows, cols = momentum.shape
    rank = prior.shape[1]
    sizes, halves, orders = stage_plan(shape, rows)
    stages = []
    now = [rows // halves] * halves
    widest = max(max(sizes.values()), shape["shard"], 2) - 1
    for level in range(3):
        for h in range(halves):
            count = sizes[orders[h][level]]
            now[h] //= count
            stages += [
                pltpu.VMEM((max(count - 1, 1), now[h], rank), jnp.float32),
                pltpu.SemaphoreType.DMA((max(count - 1, 1),)),
                pltpu.SemaphoreType.DMA((max(count - 1, 1),)),
            ]
    z = shape["shard"]
    plane = shape["tensor"] * shape["dp"]
    dma = pltpu.SemaphoreType.DMA
    vmem = pl.BlockSpec(memory_space=pltpu.VMEM)
    anywhere = pl.BlockSpec(memory_space=pl.ANY)
    f32 = jnp.float32
    basis, right, following = pl.pallas_call(
        functools.partial(factors, shape),
        out_shape=[
            jax.ShapeDtypeStruct((rows, rank), f32),
            jax.ShapeDtypeStruct((cols, rank), f32),
            jax.ShapeDtypeStruct((cols, rank), f32),
        ],
        in_specs=[anywhere, anywhere, vmem],
        out_specs=[vmem, vmem, vmem],
        scratch_shapes=[
            pltpu.VMEM((rows, cols), f32),
            pltpu.VMEM((rows, cols), jnp.bfloat16),
            pltpu.VMEM((rows, rank), f32),
            pltpu.VMEM((rows, rank), f32),
            pltpu.VMEM((rank, cols), f32),
            pltpu.VMEM((2, plane, rank // plane, rank), f32),
            pltpu.VMEM((2, plane, rank // plane, rank), f32),
            pltpu.VMEM((2, z, rank // plane, rank), f32),
            pltpu.VMEM((2, plane, rank // plane, rank), f32),
            pltpu.VMEM((z, rank // z, cols), f32),
            pltpu.VMEM((max(z - 1, 1), rank // z, cols), f32),
            pltpu.VMEM((plane, 8, rank), f32),
            dma((2, CHUNKS)),
            dma((2, 3, max(plane, z))),
            dma((2, 3, max(plane, z))),
            dma((max(z - 1, 1),)),
            dma((max(z - 1, 1),)),
            dma((3 * halves + 1, widest)),
            dma((3 * halves + 1, widest)),
            dma((max(plane - 1, 1),)),
            dma((max(plane - 1, 1),)),
            *stages,
        ],
        compiler_params=pltpu.CompilerParams(
            collective_id=0, has_side_effects=True, vmem_limit_bytes=48 * 1024 * 1024
        ),
        name="factors",
    )(momentum, gradient, prior)

    block = rows // CHUNKS
    wide = pl.BlockSpec((block, cols), lambda i: (i, 0))
    whole = pl.BlockSpec((cols, rank), lambda i: (0, 0))
    scale = float((rows * z / rank) ** 0.5)
    momentum_next, direction = pl.pallas_call(
        functools.partial(finish, scale),
        grid=(CHUNKS,),
        out_shape=[
            jax.ShapeDtypeStruct((rows, cols), f32),
            jax.ShapeDtypeStruct((rows, cols), jnp.bfloat16),
        ],
        in_specs=[wide, wide, pl.BlockSpec((block, rank), lambda i: (i, 0)), whole, whole],
        out_specs=[wide, wide],
        name="finish",
    )(momentum, gradient, basis, right, following)
    return momentum_next[None], following[None], direction[None]


def solution(mesh):
    return jax.shard_map(
        functools.partial(shards, dict(mesh.shape)),
        mesh=mesh,
        in_specs=(
            P(None, "shard", ("tensor", "dp")),
            P(None, "shard", ("tensor", "dp")),
            P(None, ("tensor", "dp"), None),
        ),
        out_specs=(
            P(None, "shard", ("tensor", "dp")),
            P(None, ("tensor", "dp"), None),
            P(None, "shard", ("tensor", "dp")),
        ),
        check_vma=False,
    )
```

```python
import functools

import jax
import jax.numpy as jnp
from jax import lax
from jax.experimental import pallas as pl
from jax.experimental.pallas import tpu as pltpu
from jax.sharding import PartitionSpec as P

MESH = pl.DeviceIdType.MESH
HIGHEST = lax.Precision.HIGHEST
decay_rate = 0.95
epsilon = 1e-06
CHUNKS = 8
STEPS = 4


def dot(a, b, dims, precision=HIGHEST):
    return lax.dot_general(
        a, b, (dims, ((), ())), precision=precision, preferred_element_type=jnp.float32
    )


def split(value):
    high = value.astype(jnp.bfloat16)
    low = (value - high.astype(jnp.float32)).astype(jnp.bfloat16)
    return high, low


def product(lhs, rhs):
    high, low = split(lhs)
    pair = jnp.concatenate(split(rhs), axis=1)
    both = dot(high, pair, ((1,), (0,)), None) + dot(low, pair, ((1,), (0,)), None)
    width = rhs.shape[1]
    return both[:, :width] + both[:, width:]


def inverse_factor(gram):
    size = gram.shape[0]
    sub = lax.broadcasted_iota(jnp.int32, (8, size), 0)
    lane = lax.broadcasted_iota(jnp.int32, (8, size), 1)
    rows = lax.broadcasted_iota(jnp.int32, (size, size), 0)
    lanes = lax.broadcasted_iota(jnp.int32, (size, size), 1)

    def row(value, index):
        return jnp.broadcast_to(value[index : index + 1], value.shape)

    def block(step, a):
        top = a[:8]
        columns = [jnp.broadcast_to(top[:, c : c + 1], (8, size)) for c in range(8)]
        panel = jnp.where(lane < 8, jnp.where(lane == sub, 1.0, 0.0), top)
        scale = jnp.zeros((8, size), jnp.float32)
        for c in range(8):
            inverse_root = lax.rsqrt(row(columns[c], c))
            scale = jnp.where(sub == c, inverse_root, scale)
            factor = jnp.where(sub > c, columns[c] * (inverse_root * inverse_root), 0.0)
            panel = panel - factor * row(panel, c)
            for j in range(c + 1, 8):
                columns[j] = columns[j] - factor * row(columns[j], c)
        square = scale * scale
        solved = panel * square
        for c in range(7, 0, -1):
            solved = solved - jnp.where(sub < c, columns[c] * square, 0.0) * row(solved, c)
        active = rows < size - 8 * step
        source = jnp.where(active, a, 0.0)[8:]
        rest = jnp.where(active & (lanes < 8), 0.0, a)[8:]
        for c in range(8):
            rest = rest - jnp.broadcast_to(source[:, c : c + 1], rest.shape) * jnp.broadcast_to(
                solved[c : c + 1], rest.shape
            )
        return pltpu.roll(jnp.concatenate([rest, panel * scale], axis=0), size - 8, 1)

    return jnp.where(rows >= lanes, lax.fori_loop(0, size // 8, block, gram), 0.0)


class Group:
    def __init__(self, count, me, where):
        self.count, self.me, self.where = count, me, where

    def peer(self, k):
        other = lax.rem(self.me + k, self.count)
        return other, self.where(other)


def groups(shape):
    s, t, d = lax.axis_index("shard"), lax.axis_index("tensor"), lax.axis_index("dp")
    tensor, dp = shape["tensor"], shape["dp"]
    cores = 2 if tensor % 2 == 0 else 1
    core, x = lax.rem(t, cores), lax.div(t, cores)
    return {
        "core": Group(cores, core, lambda j: {"tensor": x * cores + j}),
        "x": Group(tensor // cores, x, lambda j: {"tensor": j * cores + core}),
        "y": Group(dp, d, lambda j: {"dp": j}),
        "z": Group(shape["shard"], s, lambda j: {"shard": j}),
        "plane": Group(
            tensor * dp, t * dp + d, lambda j: {"tensor": lax.div(j, dp), "dp": lax.rem(j, dp)}
        ),
    }


def stage_plan(shape, rows):
    cores = 2 if shape["tensor"] % 2 == 0 else 1
    sizes = {"core": cores, "x": shape["tensor"] // cores, "y": shape["dp"]}
    members = shape["tensor"] * shape["dp"]
    halves = 2 if rows % (16 * members) == 0 else 1
    orders = (("core", "x", "y"), ("core", "y", "x"))[:halves]
    return sizes, halves, orders


def factors(shape, momentum_ref, gradient_ref, prior_ref, basis_ref, right_ref, following_ref, *scratch):
    (mixed, raw, left, whole, local, pieces, piece_in, piece_z, piece_all, shares, share_in, squares, load_sem,
     gram_send, gram_recv, share_send,
     share_recv, full_send, full_recv, square_send, square_recv, prior_vmem,
     prior_sem, *stages) = scratch
    rows, cols = mixed.shape
    rank = prior_ref.shape[1]
    where = groups(shape)
    sizes, halves, orders = stage_plan(shape, rows)
    part = rows // CHUNKS

    def load(i):
        at = pl.ds(pl.multiple_of(i * part, 8), part)
        return (
            pltpu.make_async_copy(momentum_ref.at[at], mixed.at[at], load_sem.at[0, i]),
            pltpu.make_async_copy(gradient_ref.at[at], raw.at[at], load_sem.at[1, i]),
        )

    prior_copy = pltpu.make_async_copy(prior_ref, prior_vmem, prior_sem)
    prior_copy.start()
    for i in range(CHUNKS):
        for copy in load(i):
            copy.start()

    barrier = pltpu.get_barrier_semaphore()
    peers = 0
    for name in ("plane", "z"):
        for k in range(1, where[name].count):
            pl.semaphore_signal(barrier, inc=1, device_id=where[name].peer(k)[1], device_id_type=MESH)
            peers += 1
    pl.semaphore_wait(barrier, peers)

    plane, z = where["plane"], where["z"]
    piece = rank // plane.count

    def summed(slots, count):
        total = slots[0]
        for i in range(1, count):
            total = total + slots[i]
        return total

    def sends(group, turn, stage, source, target):
        copies = []
        for k in range(1, group.count):
            other, device = group.peer(k)
            copy = pltpu.make_async_remote_copy(
                src_ref=source(other),
                dst_ref=target,
                send_sem=gram_send.at[turn, stage, k - 1],
                recv_sem=gram_recv.at[turn, stage, k - 1],
                device_id=device,
                device_id_type=MESH,
            )
            copy.start()
            copies.append(copy)
        return copies

    def gram_steps(turn, values):
        gram = sum(dot(value, value, ((0,), (0,))) for value in values)
        for i in range(plane.count):
            pieces[turn, i] = gram[i * piece : (i + 1) * piece]
        piece_in[turn, plane.me] = pieces[turn, plane.me]
        copies = sends(plane, turn, 0, lambda i: pieces.at[turn, i], piece_in.at[turn, plane.me])
        yield
        for copy in copies:
            copy.wait()
        piece_z[turn, z.me] = summed(piece_in.at[turn], plane.count)
        own = piece_z.at[turn, z.me]
        copies = sends(z, turn, 1, lambda i: own, own)
        yield
        for copy in copies:
            copy.wait()
        piece_all[turn, plane.me] = summed(piece_z.at[turn], z.count)
        own = piece_all.at[turn, plane.me]
        copies = sends(plane, turn, 2, lambda i: own, own)
        yield
        for copy in copies:
            copy.wait()
        yield jnp.concatenate([piece_all[turn, i] for i in range(plane.count)], axis=0)

    prior_copy.wait()
    prior = prior_vmem[...]

    def first(i, carry):
        for copy in load(i):
            copy.wait()
        at = pl.ds(pl.multiple_of(i * part, 8), part)
        value = mixed[at, :] + raw[at, :].astype(jnp.float32)
        mixed[at, :] = value
        left[at, :] = product(value, prior)
        return carry

    lax.fori_loop(0, CHUNKS, first, 0)

    starts = [h * (rows // halves) for h in range(halves)]
    sizes_now = [rows // halves] * halves
    trail = []
    for level in range(3):
        pending = []
        for h in range(halves):
            name = orders[h][level]
            group = where[name]
            buffer, send_sem, recv_sem = stages[level * 6 + h * 3 : level * 6 + h * 3 + 3] if halves == 2 else stages[level * 3 : level * 3 + 3]
            if group.count == 1:
                continue
            size = sizes_now[h] // group.count
            copies = []
            for k in range(1, group.count):
                other, device = group.peer(k)
                copy = pltpu.make_async_remote_copy(
                    src_ref=left.at[pl.ds(pl.multiple_of(starts[h] + other * size, 8), size)],
                    dst_ref=buffer.at[k - 1],
                    send_sem=send_sem.at[k - 1],
                    recv_sem=recv_sem.at[k - 1],
                    device_id=device,
                    device_id_type=MESH,
                )
                copy.start()
                copies.append(copy)
            pending.append((h, group, size, copies, buffer))
        for h, group, size, copies, buffer in pending:
            for copy in copies:
                copy.wait()
            own = pl.multiple_of(starts[h] + group.me * size, 8)
            total = left[pl.ds(own, size), :]
            for k in range(group.count - 1):
                total = total + buffer[k]
            left[pl.ds(own, size), :] = total
            starts[h], sizes_now[h] = own, size
            trail.append((level, h, group, own, size))
    for h in range(halves):
        own = pl.ds(starts[h], sizes_now[h])
        whole[own, :] = left[own, :]
    for level in (2, 1, 0):
        copies = []
        for stage, h, group, own, size in trail:
            if stage != level:
                continue
            index = (level * 2 + h) if halves == 2 else level
            for k in range(1, group.count):
                other, device = group.peer(k)
                at = pl.ds(own, size)
                copy = pltpu.make_async_remote_copy(
                    src_ref=whole.at[at],
                    dst_ref=whole.at[at],
                    send_sem=full_send.at[index, k - 1],
                    recv_sem=full_recv.at[index, k - 1],
                    device_id=device,
                    device_id_type=MESH,
                )
                copy.start()
                copies.append(copy)
        if level == 2:
            steps = gram_steps(0, [left[pl.ds(starts[h], sizes_now[h]), :] for h in range(halves)])
            next(steps)
        elif level == 1:
            next(steps)
        else:
            next(steps)
            inverse = inverse_factor(next(steps))
            owned = [
                dot(left[pl.ds(starts[h], sizes_now[h]), :], inverse, ((1,), (1,))) for h in range(halves)
            ]
            steps = gram_steps(1, owned)
            next(steps)
        for copy in copies:
            copy.wait()

    def exchange(slots, group, send_sem, recv_sem):
        copies = []
        for k in range(1, group.count):
            copy = pltpu.make_async_remote_copy(
                src_ref=slots.at[group.me],
                dst_ref=slots.at[group.me],
                send_sem=send_sem.at[k - 1],
                recv_sem=recv_sem.at[k - 1],
                device_id=group.peer(k)[1],
                device_id_type=MESH,
            )
            copy.start()
            copies.append(copy)
        return copies

    value = dot(whole[...], inverse, ((1,), (1,)))
    basis_ref[...] = value
    next(steps)
    high, low = split(value)
    half = cols // 2
    for c in range(2):
        wide_high, wide_low = split(mixed[:, c * half : (c + 1) * half])
        both = dot(jnp.concatenate([high, low], axis=1), wide_high, ((0,), (0,)), None)
        local[:, c * half : (c + 1) * half] = (
            both[:rank] + both[rank:] + dot(high, wide_low, ((0,), (0,)), None)
        )
        if c == 0:
            next(steps)
    share = rank // z.count
    share_copies = []
    for k in range(1, z.count):
        other, device = z.peer(k)
        copy = pltpu.make_async_remote_copy(
            src_ref=local.at[pl.ds(pl.multiple_of(other * share, 8), share)],
            dst_ref=share_in.at[k - 1],
            send_sem=share_send.at[k - 1],
            recv_sem=share_recv.at[k - 1],
            device_id=device,
            device_id_type=MESH,
        )
        copy.start()
        share_copies.append(copy)
    inverse = inverse_factor(next(steps))
    for copy in share_copies:
        copy.wait()
    total = local[pl.ds(pl.multiple_of(z.me * share, 8), share), :]
    for k in range(z.count - 1):
        total = total + share_in[k]
    shares[z.me] = total
    full = exchange(shares, z, full_send.at[full_send.shape[0] - 1], full_recv.at[full_recv.shape[0] - 1])
    basis_ref[...] = dot(basis_ref[...], inverse, ((1,), (1,)))
    for copy in full:
        copy.wait()
    stacked = jnp.concatenate([shares[i] for i in range(z.count)], axis=0)
    right = dot(stacked, inverse, ((0,), (1,)))
    right_ref[...] = right
    squares[plane.me] = jnp.broadcast_to(jnp.sum(right * right, axis=0, keepdims=True), (8, rank))
    for copy in exchange(squares, plane, square_send, square_recv):
        copy.wait()
    mean = summed(squares, plane.count)[:1] / (cols * plane.count)
    following_ref[...] = right / jnp.sqrt(mean + epsilon)


def finish(scale, momentum_ref, gradient_ref, basis_ref, right_ref, following_ref, next_ref, direction_ref):
    high, low = split(basis_ref[...])
    right = right_ref[...].astype(jnp.bfloat16)
    follow_high, follow_low = split(following_ref[...])
    dims = ((1,), (1,))
    next_ref[...] = (
        momentum_ref[...]
        + gradient_ref[...].astype(jnp.float32)
        - (1.0 - decay_rate) * dot(high, right, dims, None)
    )
    product = dot(
        jnp.concatenate([high, low], axis=1), jnp.concatenate([follow_high, follow_high], axis=1), dims, None
    ) + dot(high, follow_low, dims, None)
    direction_ref[...] = (scale * product).astype(jnp.bfloat16)


def shards(shape, gradient, momentum, prior_right_factor):
    gradient, momentum, prior = gradient[0], momentum[0], prior_right_factor[0]
    rows, cols = momentum.shape
    rank = prior.shape[1]
    sizes, halves, orders = stage_plan(shape, rows)
    stages = []
    now = [rows // halves] * halves
    widest = max(max(sizes.values()), shape["shard"], 2) - 1
    for level in range(3):
        for h in range(halves):
            count = sizes[orders[h][level]]
            now[h] //= count
            stages += [
                pltpu.VMEM((max(count - 1, 1), now[h], rank), jnp.float32),
                pltpu.SemaphoreType.DMA((max(count - 1, 1),)),
                pltpu.SemaphoreType.DMA((max(count - 1, 1),)),
            ]
    z = shape["shard"]
    plane = shape["tensor"] * shape["dp"]
    dma = pltpu.SemaphoreType.DMA
    vmem = pl.BlockSpec(memory_space=pltpu.VMEM)
    anywhere = pl.BlockSpec(memory_space=pl.ANY)
    f32 = jnp.float32
    basis, right, following = pl.pallas_call(
        functools.partial(factors, shape),
        out_shape=[
            jax.ShapeDtypeStruct((rows, rank), f32),
            jax.ShapeDtypeStruct((cols, rank), f32),
            jax.ShapeDtypeStruct((cols, rank), f32),
        ],
        in_specs=[anywhere, anywhere, anywhere],
        out_specs=[vmem, vmem, vmem],
        scratch_shapes=[
            pltpu.VMEM((rows, cols), f32),
            pltpu.VMEM((rows, cols), jnp.bfloat16),
            pltpu.VMEM((rows, rank), f32),
            pltpu.VMEM((rows, rank), f32),
            pltpu.VMEM((rank, cols), f32),
            pltpu.VMEM((2, plane, rank // plane, rank), f32),
            pltpu.VMEM((2, plane, rank // plane, rank), f32),
            pltpu.VMEM((2, z, rank // plane, rank), f32),
            pltpu.VMEM((2, plane, rank // plane, rank), f32),
            pltpu.VMEM((z, rank // z, cols), f32),
            pltpu.VMEM((max(z - 1, 1), rank // z, cols), f32),
            pltpu.VMEM((plane, 8, rank), f32),
            dma((2, CHUNKS)),
            dma((2, 3, max(plane, z))),
            dma((2, 3, max(plane, z))),
            dma((max(z - 1, 1),)),
            dma((max(z - 1, 1),)),
            dma((3 * halves + 1, widest)),
            dma((3 * halves + 1, widest)),
            dma((max(plane - 1, 1),)),
            dma((max(plane - 1, 1),)),
            pltpu.VMEM((cols, rank), f32),
            dma,
            *stages,
        ],
        compiler_params=pltpu.CompilerParams(
            collective_id=0, has_side_effects=True, vmem_limit_bytes=48 * 1024 * 1024
        ),
        name="factors",
    )(momentum, gradient, prior)

    block = rows // STEPS
    wide = pl.BlockSpec((block, cols), lambda i: (i, 0))
    whole = pl.BlockSpec((cols, rank), lambda i: (0, 0))
    scale = float((rows * z / rank) ** 0.5)
    momentum_next, direction = pl.pallas_call(
        functools.partial(finish, scale),
        grid=(STEPS,),
        out_shape=[
            jax.ShapeDtypeStruct((rows, cols), f32),
            jax.ShapeDtypeStruct((rows, cols), jnp.bfloat16),
        ],
        in_specs=[wide, wide, pl.BlockSpec((block, rank), lambda i: (i, 0)), whole, whole],
        out_specs=[wide, wide],
        name="finish",
    )(momentum, gradient, basis, right, following)
    return momentum_next[None], following[None], direction[None]


def solution(mesh):
    return jax.shard_map(
        functools.partial(shards, dict(mesh.shape)),
        mesh=mesh,
        in_specs=(
            P(None, "shard", ("tensor", "dp")),
            P(None, "shard", ("tensor", "dp")),
            P(None, ("tensor", "dp"), None),
        ),
        out_specs=(
            P(None, "shard", ("tensor", "dp")),
            P(None, ("tensor", "dp"), None),
            P(None, "shard", ("tensor", "dp")),
        ),
        check_vma=False,
    )
```
